128 devices in a mesh: dp: 4 (over x), expert: 32 (over z, y, core).
Axes of the slice: x: 4, y: 4, z: 4, core: 2. Of those that a mesh axis runs over, the one named last changes fastest.
Arguments:
- tokens: bfloat16 [10240, 7168], P('expert', 'dp'), may hold values from -6 to 6
- route_ids: int32 [10240, 8], P('expert'), may hold values from 0 to 255, as said below
- route_scores: float32 [10240, 8], P('expert'), may hold values from 0.05 to 1
- partner: int32 [32], replicated, may hold values from 0 to 31, as said below
- w_gate: bfloat16 [32, 7168, 1024], P('expert', None, 'dp'), may hold values from -0.0625 to 0.0625
- w_up: bfloat16 [32, 7168, 1024], P('expert', None, 'dp'), may hold values from -0.0625 to 0.0625
- w_down: bfloat16 [32, 1024, 7168], P('expert', 'dp'), may hold values from -0.5 to 0.5
Outputs:
- mixed: bfloat16 [10240, 7168], P('expert', 'dp')
- placed_gate: bfloat16 [32, 7168, 1024], P('expert', None, 'dp')
- placed_up: bfloat16 [32, 7168, 1024], P('expert', None, 'dp')
- placed_down: bfloat16 [32, 1024, 7168], P('expert', 'dp')
The draws below stay inside these ranges and needn't reach their ends.
Inputs may be any that keep to these rules, and one draw needn't show every extreme that they name: `route_ids`: each token names 8 different experts, exactly one of them below 32. The 320 tokens of one index of expert name each expert below 32 at most 20 times, and one expert below 32 is named exactly 20 times by the tokens of every index. partner[e] is e or e xor 1, and partner[partner[e]] = e.
All inputs are finite; a program needn't handle non-finite values.
Results may differ from the reference program's by a relative error of at most 0.017.
Values may be sent and summed in bfloat16 or wider, within the bound.
No kernel may reach another device: no remote copies, remote signals or barrier semaphores. Data moves between devices by JAX's collectives and lax.ppermute only.
A program may use at most 192 MiB of HBM per device.

```python
import jax
import jax.numpy as jnp
from jax import lax

D = 7168
MI = 1024
ROUTED = 256
TOP = 8
TOK_DEV = 320
EXPERTS = 32
CAP = 20
TOKENS = 10240
N_DP = 4


def draw_route_ids(key, part):
    key_full, key_pool, key_base, key_offset, key_column = jax.random.split(key, 5)
    full_expert = jax.random.randint(key_full, (), 0, EXPERTS)
    others = jnp.arange(EXPERTS - 1, dtype=jnp.int32)
    others = others + (others >= full_expert).astype(jnp.int32)
    slot_pool = jnp.repeat(others, CAP)

    def one_block(block_key):
        first_key, second_key = jax.random.split(block_key)
        chosen = jax.random.permutation(first_key, slot_pool)[:TOK_DEV - CAP]
        listed = jnp.concatenate([jnp.full((CAP,), full_expert, jnp.int32), chosen])
        return jax.random.permutation(second_key, listed)
    window_ids = jax.vmap(one_block)(jax.random.split(key_pool, EXPERTS)).reshape(TOKENS)
    span_width = ROUTED - EXPERTS
    step_width = span_width // (TOP - 1)
    base_pick = jax.random.randint(key_base, (TOKENS, 1), 0, span_width)
    offsets = jax.random.randint(key_offset, (TOKENS, TOP - 1), 0, step_width)
    outer_ids = EXPERTS + (base_pick + jnp.arange(TOP - 1, dtype=jnp.int32)[None, :] * step_width + offsets) % span_width
    window_column = jax.random.randint(key_column, (TOKENS, 1), 0, TOP)
    columns = jnp.arange(TOP, dtype=jnp.int32)[None, :]
    source_column = jnp.clip(columns - (columns > window_column).astype(jnp.int32), 0, TOP - 2)
    rest_ids = jnp.take_along_axis(outer_ids, jnp.broadcast_to(source_column, (TOKENS, TOP)), axis=1)
    return jnp.where(columns == window_column, window_ids[:, None], rest_ids).astype(jnp.int32)


def draw_partner(key, part):
    pair_flags = jax.random.randint(key, (EXPERTS // 2,), 0, 2).astype(jnp.int32)
    pair_flags = jnp.repeat(pair_flags, 2)
    return (jnp.arange(EXPERTS, dtype=jnp.int32) ^ pair_flags).astype(jnp.int32)


def shard_levels(own_key, dims, cuts, smallest, largest):
    def one(dim, parts):
        steps = jax.random.uniform(jax.random.fold_in(jax.random.fold_in(own_key, 6), dim), (parts,), jnp.float32, smallest / len(cuts), largest / len(cuts))
        return jnp.repeat(jnp.exp(steps), dims[dim] // parts).reshape((-1,) + (1,) * (len(dims) - dim - 1))

    loudness = one(*cuts[0])
    for cut in cuts[1:]:
        loudness = loudness * one(*cut)
    return loudness


def noise(own_key, extent, scale, bound, cuts=(), kind=jnp.bfloat16):
    entries = scale * jax.random.normal(own_key, extent, jnp.float32)
    if cuts:
        entries = entries * shard_levels(own_key, extent, cuts, -0.22, 0.18)
    return jnp.clip(entries, -bound, bound).astype(kind)


def setup_inputs(seed: int = 0) -> dict:
    key_of = jax.random.split(jax.random.key(seed), 8)
    tokens = noise(key_of[0], (TOKENS, D), 1.0, 6.0, ((0, 32), (1, 4)))
    route_ids = draw_route_ids(jax.random.fold_in(key_of[7], 71), 0)
    route_scores = jnp.clip(0.05 + 0.95 * jax.random.uniform(key_of[2], (TOKENS, TOP), jnp.float32) ** shard_levels(key_of[2], (TOKENS, TOP), ((0, 32),), -0.2, 0.2), 0.05, 1.0)
    partner = draw_partner(jax.random.fold_in(key_of[7], 71), 0)
    w_gate = noise(key_of[4], (EXPERTS, D, MI), D ** -0.5, 0.0625, ((0, 32), (2, 4)))
    w_up = noise(key_of[5], (EXPERTS, D, MI), D ** -0.5, 0.0625, ((0, 32), (2, 4)))
    w_down = noise(key_of[6], (EXPERTS, MI, D), (MI // 8) ** -0.5, 0.5, ((0, 32), (1, 4)))
    return {"tokens": tokens, "route_ids": route_ids, "route_scores": route_scores, "partner": partner, "w_gate": w_gate, "w_up": w_up, "w_down": w_down}


def reference(tokens, route_ids, route_scores, partner, w_gate, w_up, w_down):
    in_window = route_ids < EXPERTS
    expert_pick = jnp.sum(jnp.where(in_window, route_ids, 0), axis=1).astype(jnp.int32)
    window_score = jnp.sum(jnp.where(in_window, route_scores, jnp.zeros_like(route_scores)), axis=1)
    gate_weight = 2.5 * window_score / jnp.sum(route_scores, axis=1)
    most_rows = CAP * EXPERTS
    group_width = MI // N_DP

    def add_expert(expert_id, totals):
        chosen = expert_pick == expert_id
        picked = jnp.nonzero(chosen, size=most_rows, fill_value=0)[0].astype(jnp.int32)
        live_rows = jnp.arange(most_rows) < jnp.sum(chosen.astype(jnp.int32))
        gathered = tokens[picked]
        gate_proj = jnp.dot(gathered, w_gate[expert_id], preferred_element_type=jnp.float32)
        up_proj = jnp.dot(gathered, w_up[expert_id], preferred_element_type=jnp.float32)
        hidden = (jax.nn.silu(gate_proj) * up_proj).astype(jnp.bfloat16)
        split_hidden = hidden.reshape(most_rows, N_DP, group_width).astype(jnp.float32)
        split_down = w_down[expert_id].reshape(N_DP, group_width, D).astype(jnp.float32)
        partial_value = jnp.einsum("mqh,qhd->qmd", split_hidden, split_down).astype(jnp.bfloat16)
        combined = jnp.sum(partial_value.astype(jnp.float32), axis=0)
        combined = jnp.where(live_rows[:, None], combined, jnp.zeros_like(combined))
        return totals.at[picked].add(combined)

    totals = lax.fori_loop(0, EXPERTS, add_expert, jnp.zeros((TOKENS, D), jnp.float32))
    mixed = (gate_weight[:, None] * totals).astype(jnp.bfloat16)
    return (mixed, w_gate[partner], w_up[partner], w_down[partner])
```

```python
import jax
import jax.numpy as jnp
from jax import lax
from jax.sharding import PartitionSpec as P

CHUNKS = (8, 12)
SEND_SLOTS = 24
CAP = 20


def shifted(value, step):
    size = lax.axis_size("dp")
    return lax.ppermute(value, "dp", [(i, (i + step) % size) for i in range(size)])


def swapped(value):
    return lax.ppermute(value, "expert", [(i, i ^ 1) for i in range(lax.axis_size("expert"))])


def dot32(left, right):
    return jnp.dot(left, right, preferred_element_type=jnp.float32)


def ring_gather(rows):
    half = rows.shape[0] // 2
    first, second = rows[:half], rows[half:]
    left_first, right_second = shifted(first, 1), shifted(second, -1)
    left_second, right_first = shifted(second, 1), shifted(first, -1)
    far_first, far_second = shifted(left_first, 1), shifted(right_second, -1)
    return (
        (first, left_first, right_first, far_first),
        (second, left_second, right_second, far_second),
    )


def body(tokens, route_ids, route_scores, partner, w_gate, w_up, w_down):
    experts = lax.axis_size("expert")
    ring = lax.axis_size("dp")
    place = lax.axis_index("dp")
    own_index = lax.axis_index("expert")
    token_rows, width = tokens.shape
    offsets = (0, -1, 1, 2)

    in_window = route_ids < experts
    expert_pick = jnp.sum(jnp.where(in_window, route_ids, 0), axis=1)
    window_score = jnp.sum(jnp.where(in_window, route_scores, jnp.zeros_like(route_scores)), axis=1)
    gate_weight = 2.5 * window_score / jnp.sum(route_scores, axis=1)
    one_hot = expert_pick[:, None] == jnp.arange(experts, dtype=jnp.int32)[None, :]
    order = jnp.arange(token_rows, dtype=jnp.int32)
    earlier = (order[:, None] > order[None, :]).astype(jnp.bfloat16)
    counts = dot32(earlier, one_hot.astype(jnp.bfloat16))
    rank = jnp.sum(jnp.where(one_hot, counts, 0.0), axis=1).astype(jnp.int32)

    def columns(offset):
        start = ((place + offset) % ring) * width
        return lax.dynamic_slice(w_down[0], (0, start), (w_down.shape[1], width))

    down = jnp.concatenate(
        [
            columns(0),
            shifted(columns(1), 1),
            shifted(columns(-1), -1),
            shifted(columns(2), 2),
        ],
        axis=0,
    )
    in_weights = []
    for offset in offsets:
        start = ((place + offset) % ring) * width
        size = (width, w_gate.shape[2])
        in_weights.append(
            jnp.concatenate(
                [
                    lax.dynamic_slice(w_gate[0], (start, 0), size),
                    lax.dynamic_slice(w_up[0], (start, 0), size),
                ],
                axis=1,
            )
        )

    slot = expert_pick * SEND_SLOTS + rank
    slots = jnp.arange(experts * SEND_SLOTS, dtype=jnp.int32)
    spread = (slots[:, None] == slot[None, :]).astype(jnp.bfloat16)
    send = dot32(spread, tokens).astype(jnp.bfloat16).reshape(experts, SEND_SLOTS, width)
    arrived = lax.all_to_all(send, "expert", split_axis=0, concat_axis=0, tiled=True)

    moved = partner[own_index] != own_index
    placed = [jnp.where(moved, swapped(w), w) for w in (w_gate, w_up, w_down)]

    total = jnp.zeros((token_rows, width), jnp.float32)
    hidden_width = w_gate.shape[2]
    low = 0
    for size in CHUNKS:
        rows = arrived[:, low : low + size].reshape(experts * size, width)
        outs = []
        hidden = []
        for shards in ring_gather(rows):
            both = sum(dot32(s, w) for s, w in zip(shards, in_weights))
            gate_proj, up_proj = both[:, :hidden_width], both[:, hidden_width:]
            hidden.append((jax.nn.silu(gate_proj) * up_proj).astype(jnp.bfloat16))
        hidden = jnp.concatenate(hidden, axis=0)
        all_hidden = jnp.concatenate(
            [hidden, shifted(hidden, 1), shifted(hidden, -1), shifted(hidden, 2)], axis=1
        )
        out = dot32(all_hidden, down).astype(jnp.bfloat16)
        back = lax.all_to_all(
            out.reshape(experts, size, width), "expert", split_axis=0, concat_axis=0, tiled=True
        ).reshape(experts * size, width)
        spot = jnp.where(
            (rank >= low) & (rank < low + size), expert_pick * size + rank - low, -1
        )
        pick = spot[:, None] == jnp.arange(experts * size, dtype=jnp.int32)[None, :]
        total = total + dot32(pick.astype(jnp.bfloat16), back)
        low += size
    mixed = (gate_weight[:, None] * total).astype(jnp.bfloat16)
    return (mixed, *placed)


def solution(mesh):
    weights = (P("expert", None, "dp"), P("expert", None, "dp"), P("expert", "dp", None))
    return jax.shard_map(
        body,
        mesh=mesh,
        in_specs=(P("expert", "dp"), P("expert", None), P("expert", None), P(), *weights),
        out_specs=(P("expert", "dp"), *weights),
        check_vma=False,
    )
```

```python
import jax
import jax.numpy as jnp
from jax import lax
from jax.sharding import PartitionSpec as P

CHUNKS = (12, 8)
SEND_SLOTS = 24
CAP = 20


def shifted(value, step):
    size = lax.axis_size("dp")
    return lax.ppermute(value, "dp", [(i, (i + step) % size) for i in range(size)])


def swapped(value):
    return lax.ppermute(value, "expert", [(i, i ^ 1) for i in range(lax.axis_size("expert"))])


def dot32(left, right):
    return jnp.dot(left, right, preferred_element_type=jnp.float32)


def body(tokens, route_ids, route_scores, partner, w_gate, w_up, w_down):
    experts = lax.axis_size("expert")
    ring = lax.axis_size("dp")
    place = lax.axis_index("dp")
    own_index = lax.axis_index("expert")
    token_rows, width = tokens.shape
    offsets = (0, -1, 1, 2)

    in_window = route_ids < experts
    expert_pick = jnp.sum(jnp.where(in_window, route_ids, 0), axis=1)
    window_score = jnp.sum(jnp.where(in_window, route_scores, jnp.zeros_like(route_scores)), axis=1)
    gate_weight = 2.5 * window_score / jnp.sum(route_scores, axis=1)
    one_hot = expert_pick[:, None] == jnp.arange(experts, dtype=jnp.int32)[None, :]
    order = jnp.arange(token_rows, dtype=jnp.int32)
    earlier = (order[:, None] > order[None, :]).astype(jnp.bfloat16)
    counts = dot32(earlier, one_hot.astype(jnp.bfloat16))
    rank = jnp.sum(jnp.where(one_hot, counts, 0.0), axis=1).astype(jnp.int32)

    def columns(offset):
        start = ((place + offset) % ring) * width
        return lax.dynamic_slice(w_down[0], (0, start), (w_down.shape[1], width))

    down = [
        columns(0),
        shifted(columns(1), 1),
        shifted(columns(-1), -1),
        shifted(columns(2), 2),
    ]
    in_weights = []
    for offset in offsets:
        start = ((place + offset) % ring) * width
        size = (width, w_gate.shape[2])
        in_weights.append(
            jnp.concatenate(
                [
                    lax.dynamic_slice(w_gate[0], (start, 0), size),
                    lax.dynamic_slice(w_up[0], (start, 0), size),
                ],
                axis=1,
            )
        )

    slot = expert_pick * SEND_SLOTS + rank
    slots = jnp.arange(experts * SEND_SLOTS, dtype=jnp.int32)
    spread = (slots[:, None] == slot[None, :]).astype(jnp.bfloat16)
    send = dot32(spread, tokens).astype(jnp.bfloat16).reshape(experts, SEND_SLOTS, width)
    arrived = lax.all_to_all(send, "expert", split_axis=0, concat_axis=0, tiled=True)
    arrived = arrived.reshape(experts * SEND_SLOTS, width)

    moved = partner[own_index] != own_index
    own = (w_gate, w_up, w_down)
    others = [swapped(w) for w in own[:2]]
    others, down = lax.optimization_barrier((others, down))
    placed = [jnp.where(moved, o, w) for o, w in zip(others, own)]
    arrived, down, placed, in_weights, w_last = lax.optimization_barrier(
        (arrived, down, placed, in_weights, w_down)
    )

    total = jnp.zeros((token_rows, width), jnp.float32)
    hidden_width = w_gate.shape[2]
    low = 0
    picks = []

    def project(parts):
        return sum(dot32(h, w) for h, w in zip(parts, down)).astype(jnp.bfloat16)

    def send_back(out, size):
        blocks = out.reshape(experts, size, width)
        back = lax.all_to_all(blocks, "expert", split_axis=0, concat_axis=0, tiled=True)
        return back.reshape(experts * size, width)

    for size in CHUNKS:
        count = experts * size
        half = count // 2
        source = jnp.arange(count, dtype=jnp.int32)
        source = source // size * SEND_SLOTS + low + source % size
        select = (source[:, None] == slots[None, :]).astype(jnp.bfloat16)
        rows = dot32(select, arrived).astype(jnp.bfloat16)
        if low:
            rows, all_hidden = lax.optimization_barrier((rows, all_hidden))
            out = project(all_hidden)
        left, right = shifted(rows, 1), shifted(rows, -1)
        left_half, right_half = left[:half], right[half:]
        if low:
            left_half, right_half, out = lax.optimization_barrier((left_half, right_half, out))
            back = send_back(out, size_before)
        far = jnp.concatenate([shifted(left_half, 1), shifted(right_half, -1)], axis=0)
        both = sum(dot32(s, w) for s, w in zip((rows, left, right, far), in_weights))
        gate_proj, up_proj = both[:, :hidden_width], both[:, hidden_width:]
        hidden = (jax.nn.silu(gate_proj) * up_proj).astype(jnp.bfloat16)
        all_hidden = (hidden, shifted(hidden, 1), shifted(hidden, -1), shifted(hidden, 2))
        spot = jnp.where(
            (rank >= low) & (rank < low + size), expert_pick * size + rank - low, -1
        )
        picks.append((spot[:, None] == jnp.arange(count, dtype=jnp.int32)[None, :]).astype(jnp.bfloat16))
        low += size
        size_before = size
        if low > size: total = total + dot32(picks[0], back)
    other = swapped(w_last)
    other, all_hidden = lax.optimization_barrier((other, all_hidden))
    out = project(all_hidden)
    other, out = lax.optimization_barrier((other, out))
    placed.append(jnp.where(moved, other, w_last))
    total = total + dot32(picks[1], send_back(out, size))
    mixed = (gate_weight[:, None] * total).astype(jnp.bfloat16)
    return (mixed, *placed)


def solution(mesh):
    weights = (P("expert", None, "dp"), P("expert", None, "dp"), P("expert", "dp", None))
    return jax.shard_map(
        body,
        mesh=mesh,
        in_specs=(P("expert", "dp"), P("expert", None), P("expert", None), P(), *weights),
        out_specs=(P("expert", "dp"), *weights),
        check_vma=False,
    )
```

```python
import jax
import jax.numpy as jnp
from jax import lax
from jax.experimental import pallas as pl
from jax.experimental.pallas import tpu as pltpu
from jax.sharding import PartitionSpec as P

CHUNKS = ((0, 12, 16), (12, 8, 8))


def tied(*values):
    return lax.optimization_barrier(values)


def shifted(value, step):
    size = lax.axis_size("dp")
    return lax.ppermute(value, "dp", [(i, (i + step) % size) for i in range(size)])


def swapped(value):
    return lax.ppermute(value, "expert", [(i, i ^ 1) for i in range(lax.axis_size("expert"))])


def dot32(left, right):
    return jnp.dot(left, right, preferred_element_type=jnp.float32)


FREE = pl.CostEstimate(flops=0, transcendentals=0, bytes_accessed=0)
LONG = pl.CostEstimate(flops=50_000_000_000, transcendentals=0, bytes_accessed=250_000_000)
PARAMS = pltpu.CompilerParams(vmem_limit_bytes=16 << 20)


def in_hbm(value):
    return pltpu.with_memory_space_constraint(value, pltpu.HBM)


def whole(shape):
    return pl.BlockSpec(shape, lambda *_: (0,) * len(shape), pipeline_mode=pl.Buffered(1))


def near_sums(shards, spots, w_gate, w_up):
    width = w_gate.shape[1] // lax.axis_size("dp")
    units = w_gate.shape[2]
    steps = len(shards)
    pieces = [piece for shard in shards for piece in shard]
    count = sum(piece.shape[0] for piece in shards[0])

    def kernel(spot_ref, *refs):
        step = pl.program_id(0)
        gate_ref, up_ref, sum_ref = refs[len(pieces) :]
        at = 0
        for i, shard in enumerate(shards):
            own = refs[at : at + len(shard)]
            at += len(shard)

            @pl.when(step == i)
            def _():
                low = 0
                for ref in own:
                    rows = ref[...]
                    span = slice(low, low + rows.shape[0])
                    low += rows.shape[0]
                    for j, weight_ref in enumerate((gate_ref, up_ref)):
                        part = dot32(rows, weight_ref[0])
                        cut = slice(j * units, (j + 1) * units)
                        sum_ref[span, cut] = part if i == 0 else sum_ref[span, cut] + part

    weight = pl.BlockSpec((1, width, units), lambda i, spot: (0, spot[i], 0))
    return pl.pallas_call(
        kernel,
        out_shape=jax.ShapeDtypeStruct((count, 2 * units), jnp.float32),
        grid_spec=pltpu.PrefetchScalarGridSpec(
            num_scalar_prefetch=1,
            grid=(steps,),
            in_specs=[whole(piece.shape) for piece in pieces] + [weight] * 2,
            out_specs=pl.BlockSpec((count, 2 * units), lambda i, spot: (0, 0)),
        ),
        compiler_params=PARAMS,
        cost_estimate=FREE,
        name="near_sums",
    )(spots, *map(in_hbm, pieces), in_hbm(w_gate), in_hbm(w_up))


def far_hidden(halves, sums, spots, w_gate, w_up):
    half, width = halves[0].shape
    units = w_gate.shape[2]
    pieces = 2
    depth = width // pieces

    def kernel(spot_ref, first_ref, second_ref, sum_ref, gate_ref, up_ref, out_ref, gates, ups):
        step = pl.program_id(0)

        @pl.when(step == 0)
        def _():
            gates[...] = sum_ref[:, :units]
            ups[...] = sum_ref[:, units:]

        for low, ref in ((0, first_ref), (half, second_ref)):
            rows = ref[...]
            gates[low : low + half] += dot32(rows, gate_ref[0])
            ups[low : low + half] += dot32(rows, up_ref[0])

        @pl.when(step == pieces - 1)
        def _():
            value = gates[...]
            out_ref[...] = (value / (1.0 + jnp.exp(-value)) * ups[...]).astype(out_ref.dtype)

    weight = pl.BlockSpec((1, depth, units), lambda i, spot: (0, spot[0] * pieces + i, 0))
    rows = pl.BlockSpec((half, depth), lambda i, spot: (0, i))
    return pl.pallas_call(
        kernel,
        out_shape=jax.ShapeDtypeStruct((2 * half, units), jnp.bfloat16),
        grid_spec=pltpu.PrefetchScalarGridSpec(
            num_scalar_prefetch=1,
            grid=(pieces,),
            in_specs=[rows, rows, whole((2 * half, 2 * units)), weight, weight],
            out_specs=pl.BlockSpec((2 * half, units), lambda i, spot: (0, 0)),
            scratch_shapes=[pltpu.VMEM((2 * half, units), jnp.float32)] * 2,
        ),
        compiler_params=PARAMS,
        cost_estimate=FREE,
        name="far_hidden",
    )(spots, *halves, sums, in_hbm(w_gate), in_hbm(w_up))


def projected(parts, down, size, held, cost):
    count, units = parts[0].shape
    steps = len(parts)
    width = down[0].shape[1]
    slots = count // size * held
    pieces = 2

    def kernel(*refs):
        hidden_refs, down_refs = refs[:steps], refs[steps : 2 * steps]
        out_ref, spread = refs[2 * steps :]

        @pl.when(pl.program_id(0) == 0)
        def _():
            if held != size:
                slot = lax.broadcasted_iota(jnp.int32, (slots, count), 0)
                row = lax.broadcasted_iota(jnp.int32, (slots, count), 1)
                source = slot // held * size + slot % held
                keep = (source == row) & (slot % held < size)
                select = jnp.where(keep, 1.0, 0.0).astype(jnp.bfloat16)
            for i, ref in enumerate(hidden_refs):
                rows = ref[...]
                if held != size:
                    rows = dot32(select, rows).astype(jnp.bfloat16)
                spread[:, i * units : (i + 1) * units] = rows

        total = dot32(spread[:, :units], down_refs[0][...])
        for i in range(1, steps):
            total += dot32(spread[:, i * units : (i + 1) * units], down_refs[i][...])
        out_ref[...] = total.astype(out_ref.dtype)

    return pl.pallas_call(
        kernel,
        out_shape=pltpu.HBM((slots, width), jnp.bfloat16),
        grid=(pieces,),
        in_specs=[whole((count, units))] * steps
        + [pl.BlockSpec((units, width // pieces), lambda i: (0, i))] * steps,
        out_specs=pl.BlockSpec((slots, width // pieces), lambda i: (0, i)),
        scratch_shapes=[pltpu.VMEM((slots, steps * units), jnp.bfloat16)],
        compiler_params=PARAMS,
        cost_estimate=cost,
        name="projected",
    )(*parts, *down)


def gate_weights(ids, scores, experts):
    count = ids.shape[0]

    def kernel(ids_ref, scores_ref, out_ref):
        value = scores_ref[...]
        inside = jnp.where(ids_ref[...] < experts, value, 0.0)
        chosen = jnp.sum(inside, axis=1, keepdims=True)
        out_ref[...] = 2.5 * chosen / jnp.sum(value, axis=1, keepdims=True)

    return pl.pallas_call(
        kernel,
        out_shape=jax.ShapeDtypeStruct((count, 1), jnp.float32),
        compiler_params=PARAMS,
        cost_estimate=LONG,
        name="gate_weights",
    )(ids, scores)


def collected(slot, back):
    count = slot.shape[0]
    slots, width = back.shape
    pieces = 2

    def kernel(slot_ref, back_ref, out_ref, pick):
        @pl.when(pl.program_id(0) == 0)
        def _():
            place = lax.broadcasted_iota(jnp.int32, (count, slots), 1)
            pick[...] = jnp.where(place == slot_ref[...], 1.0, 0.0).astype(jnp.bfloat16)

        out_ref[...] = dot32(pick[...], back_ref[...])

    return pl.pallas_call(
        kernel,
        out_shape=jax.ShapeDtypeStruct((count, width), jnp.float32),
        grid=(pieces,),
        in_specs=[whole((count, 1)), pl.BlockSpec((slots, width // pieces), lambda i: (0, i))],
        out_specs=pl.BlockSpec((count, width // pieces), lambda i: (0, i)),
        scratch_shapes=[pltpu.VMEM((count, slots), jnp.bfloat16)],
        compiler_params=PARAMS,
        cost_estimate=LONG,
        name="collected",
    )(slot, in_hbm(back))


def exchanged(rows):
    experts = lax.axis_size("expert")
    blocks = rows.reshape(experts, rows.shape[0] // experts, rows.shape[1])
    got = lax.all_to_all(blocks, "expert", split_axis=0, concat_axis=0, tiled=True)
    return got.reshape(rows.shape)


def matches(left, right):
    return (left[:, None] == right[None, :]).astype(jnp.bfloat16)


def body(tokens, route_ids, route_scores, partner, w_gate, w_up, w_down):
    experts = lax.axis_size("expert")
    ring = lax.axis_size("dp")
    place = lax.axis_index("dp")
    own_index = lax.axis_index("expert")
    token_rows, width = tokens.shape
    hidden_width = w_gate.shape[2]
    moved = partner[own_index] != own_index

    in_window = route_ids < experts
    expert_pick = jnp.sum(jnp.where(in_window, route_ids, 0), axis=1)
    one_hot = expert_pick[:, None] == jnp.arange(experts, dtype=jnp.int32)[None, :]
    order = jnp.arange(token_rows, dtype=jnp.int32)
    earlier = (order[:, None] > order[None, :]).astype(jnp.bfloat16)
    counts = dot32(earlier, one_hot.astype(jnp.bfloat16))
    rank = jnp.sum(jnp.where(one_hot, counts, 0.0), axis=1).astype(jnp.int32)

    def send_rows(chunk, source):
        low, size, held = chunk
        inside = (rank >= low) & (rank < low + size)
        slot = jnp.where(inside, expert_pick * held + rank - low, -1)
        slots = jnp.arange(experts * held, dtype=jnp.int32)
        return dot32(matches(slots, slot), source).astype(jnp.bfloat16), slot

    def live_rows(chunk, got):
        low, size, held = chunk
        if size == held:
            return got
        rows = jnp.arange(experts * size, dtype=jnp.int32)
        slots = jnp.arange(experts * held, dtype=jnp.int32)
        return dot32(matches(rows // size * held + rows % size, slots), got).astype(jnp.bfloat16)

    def columns(offset):
        start = ((place + offset) % ring) * width
        return lax.dynamic_slice(w_down[0], (0, start), (w_down.shape[1], width))

    send_a, slot_a = send_rows(CHUNKS[0], tokens)
    send_a, gate_own, up_own = tied(send_a, w_gate, w_up)
    got_a = exchanged(send_a)

    down = [
        columns(0),
        shifted(columns(1), 1),
        shifted(columns(-1), -1),
        shifted(columns(2), 2),
    ]
    swaps = [swapped(w_gate), swapped(w_up)]
    swaps, down, scores = tied(swaps, down, route_scores)
    gate_weight = gate_weights(route_ids, scores, experts)
    got_a, down, tokens, gate_weight, swaps, own = tied(
        got_a, down, tokens, gate_weight, swaps, (w_gate, w_up, w_down)
    )
    send_b, slot_b = send_rows(CHUNKS[1], tokens)
    got_b = exchanged(send_b)

    def split(rows):
        half = rows.shape[0] // 2
        return rows[:half], rows[half:]

    def first_step(halves):
        return shifted(halves[0], 1), shifted(halves[1], -1)

    spots = [(place + offset) % ring for offset in (0, -1, 1, 2)]
    near_spots = jnp.stack(spots[:3]).astype(jnp.int32)
    far_spots = jnp.stack(spots[3:]).astype(jnp.int32)

    def activations(halves, near):
        far = first_step(near)
        left = (near[0], shifted(halves[1], 1))
        right = (shifted(halves[0], -1), near[1])
        sums = near_sums((halves, left, right), near_spots, gate_own, up_own)
        hidden = far_hidden(far, sums, far_spots, gate_own, up_own)
        return [hidden, shifted(hidden, 1), shifted(hidden, -1), shifted(hidden, 2)]

    def project(chunk, hidden, cost):
        return projected(hidden, down, chunk[1], chunk[2], cost)

    halves_a = split(live_rows(CHUNKS[0], got_a))
    hidden_a = activations(halves_a, first_step(halves_a))
    halves_b = split(live_rows(CHUNKS[1], got_b))
    halves_b, hidden_a = tied(halves_b, hidden_a)
    near = first_step(halves_b)
    out_a = project(CHUNKS[0], hidden_a, LONG)
    near, out_a = tied(near, out_a)
    back_a = exchanged(out_a)
    hidden_b = activations(halves_b, near)
    other = swapped(own[2])
    total, hidden_b = tied(collected(slot_a[:, None], back_a), hidden_b)
    out_b = project(CHUNKS[1], hidden_b, FREE)
    swaps, other, out_b, own = tied(swaps, other, out_b, own)
    placed = [jnp.where(moved, o, w) for o, w in zip((*swaps, other), own)]
    back_b = exchanged(out_b)
    slots = jnp.arange(back_b.shape[0], dtype=jnp.int32)
    total = total + dot32(matches(slot_b, slots), back_b)
    mixed = (gate_weight * total).astype(jnp.bfloat16)
    return (mixed, *placed)


def solution(mesh):
    weights = (P("expert", None, "dp"), P("expert", None, "dp"), P("expert", "dp", None))
    return jax.shard_map(
        body,
        mesh=mesh,
        in_specs=(P("expert", "dp"), P("expert", None), P("expert", None), P(), *weights),
        out_specs=(P("expert", "dp"), *weights),
        check_vma=False,
    )
```

```python
import jax
import jax.numpy as jnp
from jax import lax
from jax.experimental import pallas as pl
from jax.experimental.pallas import tpu as pltpu
from jax.sharding import PartitionSpec as P

CHUNKS = ((0, 12, 16), (12, 8, 8))


def tied(*values):
    return lax.optimization_barrier(values)


def shifted(value, step):
    size = lax.axis_size("dp")
    return lax.ppermute(value, "dp", [(i, (i + step) % size) for i in range(size)])


def swapped(value):
    return lax.ppermute(value, "expert", [(i, i ^ 1) for i in range(lax.axis_size("expert"))])


def dot32(left, right):
    return jnp.dot(left, right, preferred_element_type=jnp.float32)


FREE = pl.CostEstimate(flops=0, transcendentals=0, bytes_accessed=0)
LONG = pl.CostEstimate(flops=50_000_000_000, transcendentals=0, bytes_accessed=250_000_000)
PARAMS = pltpu.CompilerParams(vmem_limit_bytes=16 << 20)


def in_hbm(value):
    return pltpu.with_memory_space_constraint(value, pltpu.HBM)


def whole(shape):
    return pl.BlockSpec(shape, lambda *_: (0,) * len(shape), pipeline_mode=pl.Buffered(1))


def near_sums(shards, spots, w_gate, w_up):
    width = w_gate.shape[1] // lax.axis_size("dp")
    units = w_gate.shape[2]
    steps = len(shards)
    pieces = [piece for shard in shards for piece in shard]
    count = sum(piece.shape[0] for piece in shards[0])

    def kernel(spot_ref, *refs):
        step = pl.program_id(0)
        gate_ref, up_ref, sum_ref = refs[len(pieces) :]
        at = 0
        for i, shard in enumerate(shards):
            own = refs[at : at + len(shard)]
            at += len(shard)

            @pl.when(step == i)
            def _():
                low = 0
                for ref in own:
                    rows = ref[...]
                    span = slice(low, low + rows.shape[0])
                    low += rows.shape[0]
                    for j, weight_ref in enumerate((gate_ref, up_ref)):
                        part = dot32(rows, weight_ref[0])
                        cut = slice(j * units, (j + 1) * units)
                        sum_ref[span, cut] = part if i == 0 else sum_ref[span, cut] + part

    weight = pl.BlockSpec((1, width, units), lambda i, spot: (0, spot[i], 0))
    return pl.pallas_call(
        kernel,
        out_shape=jax.ShapeDtypeStruct((count, 2 * units), jnp.float32),
        grid_spec=pltpu.PrefetchScalarGridSpec(
            num_scalar_prefetch=1,
            grid=(steps,),
            in_specs=[whole(piece.shape) for piece in pieces] + [weight] * 2,
            out_specs=pl.BlockSpec((count, 2 * units), lambda i, spot: (0, 0)),
        ),
        compiler_params=PARAMS,
        cost_estimate=FREE,
        name="near_sums",
    )(spots, *pieces, in_hbm(w_gate), in_hbm(w_up))


def far_hidden(halves, sums, spots, w_gate, w_up):
    half, width = halves[0].shape
    units = w_gate.shape[2]
    pieces = 2
    depth = width // pieces

    def kernel(spot_ref, first_ref, second_ref, sum_ref, gate_ref, up_ref, out_ref, gates, ups):
        step = pl.program_id(0)

        @pl.when(step == 0)
        def _():
            gates[...] = sum_ref[:, :units]
            ups[...] = sum_ref[:, units:]

        for low, ref in ((0, first_ref), (half, second_ref)):
            rows = ref[...]
            gates[low : low + half] += dot32(rows, gate_ref[0])
            ups[low : low + half] += dot32(rows, up_ref[0])

        @pl.when(step == pieces - 1)
        def _():
            value = gates[...]
            out_ref[...] = (value / (1.0 + jnp.exp(-value)) * ups[...]).astype(out_ref.dtype)

    weight = pl.BlockSpec((1, depth, units), lambda i, spot: (0, spot[0] * pieces + i, 0))
    rows = pl.BlockSpec((half, depth), lambda i, spot: (0, i))
    return pl.pallas_call(
        kernel,
        out_shape=jax.ShapeDtypeStruct((2 * half, units), jnp.bfloat16),
        grid_spec=pltpu.PrefetchScalarGridSpec(
            num_scalar_prefetch=1,
            grid=(pieces,),
            in_specs=[rows, rows, whole((2 * half, 2 * units)), weight, weight],
            out_specs=pl.BlockSpec((2 * half, units), lambda i, spot: (0, 0)),
            scratch_shapes=[pltpu.VMEM((2 * half, units), jnp.float32)] * 2,
        ),
        compiler_params=PARAMS,
        cost_estimate=FREE,
        name="far_hidden",
    )(spots, *halves, sums, in_hbm(w_gate), in_hbm(w_up))


def projected(parts, down, size, held, cost):
    count, units = parts[0].shape
    steps = len(parts)
    width = down[0].shape[1]
    slots = count // size * held
    pieces = 2

    def kernel(*refs):
        hidden_refs, down_refs = refs[:steps], refs[steps : 2 * steps]
        out_ref, spread = refs[2 * steps :]

        @pl.when(pl.program_id(0) == 0)
        def _():
            if held != size:
                slot = lax.broadcasted_iota(jnp.int32, (slots, count), 0)
                row = lax.broadcasted_iota(jnp.int32, (slots, count), 1)
                source = slot // held * size + slot % held
                keep = (source == row) & (slot % held < size)
                select = jnp.where(keep, 1.0, 0.0).astype(jnp.bfloat16)
            for i, ref in enumerate(hidden_refs):
                rows = ref[...]
                if held != size:
                    rows = dot32(select, rows).astype(jnp.bfloat16)
                spread[:, i * units : (i + 1) * units] = rows

        total = dot32(spread[:, :units], down_refs[0][...])
        for i in range(1, steps):
            total += dot32(spread[:, i * units : (i + 1) * units], down_refs[i][...])
        out_ref[...] = total.astype(out_ref.dtype)

    return pl.pallas_call(
        kernel,
        out_shape=pltpu.HBM((slots, width), jnp.bfloat16),
        grid=(pieces,),
        in_specs=[whole((count, units))] * steps
        + [pl.BlockSpec((units, width // pieces), lambda i: (0, i))] * steps,
        out_specs=pl.BlockSpec((slots, width // pieces), lambda i: (0, i)),
        scratch_shapes=[pltpu.VMEM((slots, steps * units), jnp.bfloat16)],
        compiler_params=PARAMS,
        cost_estimate=cost,
        name="projected",
    )(*parts, *down)


def gate_weights(ids, scores, experts):
    count = ids.shape[0]

    def kernel(ids_ref, scores_ref, out_ref):
        value = scores_ref[...]
        inside = jnp.where(ids_ref[...] < experts, value, 0.0)
        chosen = jnp.sum(inside, axis=1, keepdims=True)
        out_ref[...] = 2.5 * chosen / jnp.sum(value, axis=1, keepdims=True)

    return pl.pallas_call(
        kernel,
        out_shape=jax.ShapeDtypeStruct((count, 1), jnp.float32),
        compiler_params=PARAMS,
        cost_estimate=LONG,
        name="gate_weights",
    )(ids, scores)


def collected(slot, back):
    count = slot.shape[0]
    slots, width = back.shape
    pieces = 2

    def kernel(slot_ref, back_ref, out_ref, pick):
        @pl.when(pl.program_id(0) == 0)
        def _():
            place = lax.broadcasted_iota(jnp.int32, (count, slots), 1)
            pick[...] = jnp.where(place == slot_ref[...], 1.0, 0.0).astype(jnp.bfloat16)

        out_ref[...] = dot32(pick[...], back_ref[...]).astype(out_ref.dtype)

    return pl.pallas_call(
        kernel,
        out_shape=pltpu.HBM((count, width), jnp.bfloat16),
        grid=(pieces,),
        in_specs=[whole((count, 1)), pl.BlockSpec((slots, width // pieces), lambda i: (0, i))],
        out_specs=pl.BlockSpec((count, width // pieces), lambda i: (0, i)),
        scratch_shapes=[pltpu.VMEM((count, slots), jnp.bfloat16)],
        compiler_params=PARAMS,
        cost_estimate=LONG,
        name="collected",
    )(slot, in_hbm(back))


def mixed_rows(slot, back, total, weight):
    count, width = total.shape
    slots = back.shape[0]
    pieces = 2

    def kernel(slot_ref, back_ref, total_ref, weight_ref, out_ref, pick):
        @pl.when(pl.program_id(0) == 0)
        def _():
            place = lax.broadcasted_iota(jnp.int32, (count, slots), 1)
            pick[...] = jnp.where(place == slot_ref[...], 1.0, 0.0).astype(jnp.bfloat16)

        rows = total_ref[...].astype(jnp.float32) + dot32(pick[...], back_ref[...])
        out_ref[...] = (weight_ref[...] * rows).astype(out_ref.dtype)

    def columns(rows):
        return pl.BlockSpec((rows, width // pieces), lambda i: (0, i))

    return pl.pallas_call(
        kernel,
        out_shape=jax.ShapeDtypeStruct((count, width), jnp.bfloat16),
        grid=(pieces,),
        in_specs=[whole((count, 1)), columns(slots), columns(count), whole((count, 1))],
        out_specs=columns(count),
        scratch_shapes=[pltpu.VMEM((count, slots), jnp.bfloat16)],
        compiler_params=PARAMS,
        cost_estimate=FREE,
        name="mixed_rows",
    )(slot, back, total, weight)


def exchanged(rows):
    experts = lax.axis_size("expert")
    blocks = rows.reshape(experts, rows.shape[0] // experts, rows.shape[1])
    got = lax.all_to_all(blocks, "expert", split_axis=0, concat_axis=0, tiled=True)
    return got.reshape(rows.shape)


def matches(left, right):
    return (left[:, None] == right[None, :]).astype(jnp.bfloat16)


def body(tokens, route_ids, route_scores, partner, w_gate, w_up, w_down):
    experts = lax.axis_size("expert")
    ring = lax.axis_size("dp")
    place = lax.axis_index("dp")
    own_index = lax.axis_index("expert")
    token_rows, width = tokens.shape
    hidden_width = w_gate.shape[2]
    moved = partner[own_index] != own_index

    in_window = route_ids < experts
    expert_pick = jnp.sum(jnp.where(in_window, route_ids, 0), axis=1)
    one_hot = expert_pick[:, None] == jnp.arange(experts, dtype=jnp.int32)[None, :]
    order = jnp.arange(token_rows, dtype=jnp.int32)
    earlier = (order[:, None] > order[None, :]).astype(jnp.bfloat16)
    counts = dot32(earlier, one_hot.astype(jnp.bfloat16))
    rank = jnp.sum(jnp.where(one_hot, counts, 0.0), axis=1).astype(jnp.int32)

    def send_rows(chunk, source):
        low, size, held = chunk
        inside = (rank >= low) & (rank < low + size)
        slot = jnp.where(inside, expert_pick * held + rank - low, -1)
        slots = jnp.arange(experts * held, dtype=jnp.int32)
        return dot32(matches(slots, slot), source).astype(jnp.bfloat16), slot

    def live_rows(chunk, got):
        low, size, held = chunk
        if size == held:
            return got
        rows = jnp.arange(experts * size, dtype=jnp.int32)
        slots = jnp.arange(experts * held, dtype=jnp.int32)
        return dot32(matches(rows // size * held + rows % size, slots), got).astype(jnp.bfloat16)

    def columns(offset):
        start = ((place + offset) % ring) * width
        return lax.dynamic_slice(w_down[0], (0, start), (w_down.shape[1], width))

    send_a, slot_a = send_rows(CHUNKS[0], tokens)
    send_a, gate_own, up_own = tied(send_a, w_gate, w_up)
    got_a = exchanged(send_a)

    down = [
        columns(0),
        shifted(columns(1), 1),
        shifted(columns(-1), -1),
        shifted(columns(2), 2),
    ]
    swaps = [swapped(w_gate), swapped(w_up)]
    swaps, down, scores = tied(swaps, down, route_scores)
    gate_weight = gate_weights(route_ids, scores, experts)
    got_a, down, tokens, gate_weight, swaps, own = tied(
        got_a, down, tokens, gate_weight, swaps, (w_gate, w_up, w_down)
    )
    send_b, slot_b = send_rows(CHUNKS[1], tokens)
    got_b = exchanged(send_b)

    def split(rows):
        half = rows.shape[0] // 2
        return rows[:half], rows[half:]

    def first_step(halves):
        return shifted(halves[0], 1), shifted(halves[1], -1)

    spots = [(place + offset) % ring for offset in (0, -1, 1, 2)]
    near_spots = jnp.stack(spots[:3]).astype(jnp.int32)
    far_spots = jnp.stack(spots[3:]).astype(jnp.int32)

    def activations(halves, near, early):
        far = first_step(near)
        left = (near[0], shifted(halves[1], 1))
        right = (shifted(halves[0], -1), near[1])
        if early:
            (left, right), early[:] = tied((left, right), early)
        sums = near_sums((halves, left, right), near_spots, gate_own, up_own)
        hidden = far_hidden(far, sums, far_spots, gate_own, up_own)
        return [hidden, shifted(hidden, 1), shifted(hidden, -1), shifted(hidden, 2)]

    def project(chunk, hidden, cost):
        return projected(hidden, down, chunk[1], chunk[2], cost)

    placed = [jnp.where(moved, o, w) for o, w in zip(swaps, own)]
    halves_a = split(live_rows(CHUNKS[0], got_a))
    hidden_a = activations(halves_a, first_step(halves_a), placed)
    halves_b = split(live_rows(CHUNKS[1], got_b))
    halves_b, hidden_a = tied(halves_b, hidden_a)
    near = first_step(halves_b)
    out_a = project(CHUNKS[0], hidden_a, LONG)
    near, out_a = tied(near, out_a)
    back_a = exchanged(out_a)
    hidden_b = activations(halves_b, near, [])
    other = swapped(own[2])
    total, hidden_b = tied(collected(slot_a[:, None], back_a), hidden_b)
    out_b = project(CHUNKS[1], hidden_b, FREE)
    other, out_b, last = tied(other, out_b, own[2])
    placed.append(jnp.where(moved, other, last))
    back_b = exchanged(out_b)
    mixed = mixed_rows(slot_b[:, None], back_b, total, gate_weight)
    return (mixed, *placed)


def solution(mesh):
    weights = (P("expert", None, "dp"), P("expert", None, "dp"), P("expert", "dp", None))
    return jax.shard_map(
        body,
        mesh=mesh,
        in_specs=(P("expert", "dp"), P("expert", None), P("expert", None), P(), *weights),
        out_specs=(P("expert", "dp"), *weights),
        check_vma=False,
    )
```

```python
import jax
import jax.numpy as jnp
from jax import lax
from jax.experimental import pallas as pl
from jax.experimental.pallas import tpu as pltpu
from jax.sharding import PartitionSpec as P

CHUNKS = ((0, 12, 16), (12, 8, 8))


def tied(*values):
    return lax.optimization_barrier(values)


def shifted(value, step):
    size = lax.axis_size("dp")
    return lax.ppermute(value, "dp", [(i, (i + step) % size) for i in range(size)])


def swapped(value):
    return lax.ppermute(value, "expert", [(i, i ^ 1) for i in range(lax.axis_size("expert"))])


def dot32(left, right):
    return jnp.dot(left, right, preferred_element_type=jnp.float32)


FREE = pl.CostEstimate(flops=0, transcendentals=0, bytes_accessed=0)
LONG = pl.CostEstimate(flops=50_000_000_000, transcendentals=0, bytes_accessed=250_000_000)
PARAMS = pltpu.CompilerParams(vmem_limit_bytes=16 << 20)


def in_hbm(value):
    return pltpu.with_memory_space_constraint(value, pltpu.HBM)


def whole(shape):
    return pl.BlockSpec(shape, lambda *_: (0,) * len(shape), pipeline_mode=pl.Buffered(1))


def near_sums(shards, spots, w_gate, w_up):
    width = w_gate.shape[1] // lax.axis_size("dp")
    units = w_gate.shape[2]
    steps = len(shards)
    pieces = [piece for shard in shards for piece in shard]
    count = sum(piece.shape[0] for piece in shards[0])

    def kernel(spot_ref, *refs):
        step = pl.program_id(0)
        gate_ref, up_ref, sum_ref = refs[len(pieces) :]
        at = 0
        for i, shard in enumerate(shards):
            own = refs[at : at + len(shard)]
            at += len(shard)

            @pl.when(step == i)
            def _():
                low = 0
                for ref in own:
                    rows = ref[...]
                    span = slice(low, low + rows.shape[0])
                    low += rows.shape[0]
                    for j, weight_ref in enumerate((gate_ref, up_ref)):
                        part = dot32(rows, weight_ref[0])
                        cut = slice(j * units, (j + 1) * units)
                        sum_ref[span, cut] = part if i == 0 else sum_ref[span, cut] + part

    weight = pl.BlockSpec((1, width, units), lambda i, spot: (0, spot[i], 0))
    return pl.pallas_call(
        kernel,
        out_shape=jax.ShapeDtypeStruct((count, 2 * units), jnp.float32),
        grid_spec=pltpu.PrefetchScalarGridSpec(
            num_scalar_prefetch=1,
            grid=(steps,),
            in_specs=[whole(piece.shape) for piece in pieces] + [weight] * 2,
            out_specs=pl.BlockSpec((count, 2 * units), lambda i, spot: (0, 0)),
        ),
        compiler_params=PARAMS,
        cost_estimate=FREE,
        name="near_sums",
    )(spots, *pieces, in_hbm(w_gate), in_hbm(w_up))


def far_hidden(halves, sums, spots, w_gate, w_up):
    half, width = halves[0].shape
    units = w_gate.shape[2]
    pieces = 2
    depth = width // pieces

    def kernel(spot_ref, first_ref, second_ref, sum_ref, gate_ref, up_ref, out_ref, gates, ups):
        step = pl.program_id(0)

        @pl.when(step == 0)
        def _():
            gates[...] = sum_ref[:, :units]
            ups[...] = sum_ref[:, units:]

        for low, ref in ((0, first_ref), (half, second_ref)):
            rows = ref[...]
            gates[low : low + half] += dot32(rows, gate_ref[0])
            ups[low : low + half] += dot32(rows, up_ref[0])

        @pl.when(step == pieces - 1)
        def _():
            value = gates[...]
            out_ref[...] = (value / (1.0 + jnp.exp(-value)) * ups[...]).astype(out_ref.dtype)

    weight = pl.BlockSpec((1, depth, units), lambda i, spot: (0, spot[0] * pieces + i, 0))
    rows = pl.BlockSpec((half, depth), lambda i, spot: (0, i))
    return pl.pallas_call(
        kernel,
        out_shape=jax.ShapeDtypeStruct((2 * half, units), jnp.bfloat16),
        grid_spec=pltpu.PrefetchScalarGridSpec(
            num_scalar_prefetch=1,
            grid=(pieces,),
            in_specs=[rows, rows, whole((2 * half, 2 * units)), weight, weight],
            out_specs=pl.BlockSpec((2 * half, units), lambda i, spot: (0, 0)),
            scratch_shapes=[pltpu.VMEM((2 * half, units), jnp.float32)] * 2,
        ),
        compiler_params=PARAMS,
        cost_estimate=FREE,
        name="far_hidden",
    )(spots, *halves, sums, in_hbm(w_gate), in_hbm(w_up))


def projected(parts, down, size, held, cost):
    count, units = parts[0].shape
    steps = len(parts)
    width = down[0].shape[1]
    slots = count // size * held
    pieces = 2

    def kernel(*refs):
        hidden_refs, down_refs = refs[:steps], refs[steps : 2 * steps]
        out_ref, spread = refs[2 * steps :]

        @pl.when(pl.program_id(0) == 0)
        def _():
            if held != size:
                slot = lax.broadcasted_iota(jnp.int32, (slots, count), 0)
                row = lax.broadcasted_iota(jnp.int32, (slots, count), 1)
                source = slot // held * size + slot % held
                keep = (source == row) & (slot % held < size)
                select = jnp.where(keep, 1.0, 0.0).astype(jnp.bfloat16)
            for i, ref in enumerate(hidden_refs):
                rows = ref[...]
                if held != size:
                    rows = dot32(select, rows).astype(jnp.bfloat16)
                spread[:, i * units : (i + 1) * units] = rows

        total = dot32(spread[:, :units], down_refs[0][...])
        for i in range(1, steps):
            total += dot32(spread[:, i * units : (i + 1) * units], down_refs[i][...])
        out_ref[...] = total.astype(out_ref.dtype)

    return pl.pallas_call(
        kernel,
        out_shape=pltpu.HBM((slots, width), jnp.bfloat16),
        grid=(pieces,),
        in_specs=[whole((count, units))] * steps
        + [pl.BlockSpec((units, width // pieces), lambda i: (0, i))] * steps,
        out_specs=pl.BlockSpec((slots, width // pieces), lambda i: (0, i)),
        scratch_shapes=[pltpu.VMEM((slots, steps * units), jnp.bfloat16)],
        compiler_params=PARAMS,
        cost_estimate=cost,
        name="projected",
    )(*parts, *down)


def gate_weights(ids, scores, experts):
    count = ids.shape[0]

    def kernel(ids_ref, scores_ref, out_ref):
        value = scores_ref[...]
        inside = jnp.where(ids_ref[...] < experts, value, 0.0)
        chosen = jnp.sum(inside, axis=1, keepdims=True)
        out_ref[...] = 2.5 * chosen / jnp.sum(value, axis=1, keepdims=True)

    return pl.pallas_call(
        kernel,
        out_shape=jax.ShapeDtypeStruct((count, 1), jnp.float32),
        compiler_params=PARAMS,
        cost_estimate=LONG,
        name="gate_weights",
    )(ids, scores)


def collected(slot, back):
    count = slot.shape[0]
    slots, width = back.shape
    pieces = 2

    def kernel(slot_ref, back_ref, out_ref, pick):
        @pl.when(pl.program_id(0) == 0)
        def _():
            place = lax.broadcasted_iota(jnp.int32, (count, slots), 1)
            pick[...] = jnp.where(place == slot_ref[...], 1.0, 0.0).astype(jnp.bfloat16)

        out_ref[...] = dot32(pick[...], back_ref[...]).astype(out_ref.dtype)

    return pl.pallas_call(
        kernel,
        out_shape=pltpu.HBM((count, width), jnp.bfloat16),
        grid=(pieces,),
        in_specs=[whole((count, 1)), pl.BlockSpec((slots, width // pieces), lambda i: (0, i))],
        out_specs=pl.BlockSpec((count, width // pieces), lambda i: (0, i)),
        scratch_shapes=[pltpu.VMEM((count, slots), jnp.bfloat16)],
        compiler_params=PARAMS,
        cost_estimate=LONG,
        name="collected",
    )(slot, in_hbm(back))


def mixed_rows(slot, back, total, weight):
    count, width = total.shape
    slots = back.shape[0]
    pieces = 2

    def kernel(slot_ref, back_ref, total_ref, weight_ref, out_ref, pick):
        @pl.when(pl.program_id(0) == 0)
        def _():
            place = lax.broadcasted_iota(jnp.int32, (count, slots), 1)
            pick[...] = jnp.where(place == slot_ref[...], 1.0, 0.0).astype(jnp.bfloat16)

        rows = total_ref[...].astype(jnp.float32) + dot32(pick[...], back_ref[...])
        out_ref[...] = (weight_ref[...] * rows).astype(out_ref.dtype)

    def columns(rows):
        return pl.BlockSpec((rows, width // pieces), lambda i: (0, i))

    return pl.pallas_call(
        kernel,
        out_shape=jax.ShapeDtypeStruct((count, width), jnp.bfloat16),
        grid=(pieces,),
        in_specs=[whole((count, 1)), columns(slots), columns(count), whole((count, 1))],
        out_specs=columns(count),
        scratch_shapes=[pltpu.VMEM((count, slots), jnp.bfloat16)],
        compiler_params=PARAMS,
        cost_estimate=FREE,
        name="mixed_rows",
    )(slot, back, total, weight)


def exchanged(rows):
    experts = lax.axis_size("expert")
    blocks = rows.reshape(experts, rows.shape[0] // experts, rows.shape[1])
    got = lax.all_to_all(blocks, "expert", split_axis=0, concat_axis=0, tiled=True)
    return got.reshape(rows.shape)


def matches(left, right):
    return (left[:, None] == right[None, :]).astype(jnp.bfloat16)


def body(tokens, route_ids, route_scores, partner, w_gate, w_up, w_down):
    experts = lax.axis_size("expert")
    ring = lax.axis_size("dp")
    place = lax.axis_index("dp")
    own_index = lax.axis_index("expert")
    token_rows, width = tokens.shape
    hidden_width = w_gate.shape[2]
    moved = partner[own_index] != own_index

    in_window = route_ids < experts
    expert_pick = jnp.sum(jnp.where(in_window, route_ids, 0), axis=1)
    one_hot = expert_pick[:, None] == jnp.arange(experts, dtype=jnp.int32)[None, :]
    order = jnp.arange(token_rows, dtype=jnp.int32)
    earlier = (order[:, None] > order[None, :]).astype(jnp.bfloat16)
    counts = dot32(earlier, one_hot.astype(jnp.bfloat16))
    rank = jnp.sum(jnp.where(one_hot, counts, 0.0), axis=1).astype(jnp.int32)

    def send_rows(chunk, source):
        low, size, held = chunk
        inside = (rank >= low) & (rank < low + size)
        slot = jnp.where(inside, expert_pick * held + rank - low, -1)
        slots = jnp.arange(experts * held, dtype=jnp.int32)
        return dot32(matches(slots, slot), source).astype(jnp.bfloat16), slot

    def live_rows(chunk, got):
        low, size, held = chunk
        if size == held:
            return got
        rows = jnp.arange(experts * size, dtype=jnp.int32)
        slots = jnp.arange(experts * held, dtype=jnp.int32)
        return dot32(matches(rows // size * held + rows % size, slots), got).astype(jnp.bfloat16)

    def columns(offset):
        start = ((place + offset) % ring) * width
        return lax.dynamic_slice(w_down[0], (0, start), (w_down.shape[1], width))

    send_a, slot_a = send_rows(CHUNKS[0], tokens)
    send_a, gate_own, up_own = tied(send_a, w_gate, w_up)
    got_a = exchanged(send_a)

    down = [
        columns(0),
        shifted(columns(1), 1),
        shifted(columns(-1), -1),
        shifted(columns(2), 2),
    ]
    swaps = [swapped(w_gate), swapped(w_up)]
    swaps, down, scores = tied(swaps, down, route_scores)
    gate_weight = gate_weights(route_ids, scores, experts)
    got_a, down, tokens, gate_weight, swaps, own = tied(
        got_a, down, tokens, gate_weight, swaps, (w_gate, w_up, w_down)
    )
    send_b, slot_b = send_rows(CHUNKS[1], tokens)
    got_b = exchanged(send_b)

    def split(rows):
        half = rows.shape[0] // 2
        return rows[:half], rows[half:]

    def first_step(halves):
        return shifted(halves[0], 1), shifted(halves[1], -1)

    spots = [(place + offset) % ring for offset in (0, -1, 1, 2)]
    near_spots = jnp.stack(spots[:3]).astype(jnp.int32)
    far_spots = jnp.stack(spots[3:]).astype(jnp.int32)

    def activations(halves, near, early):
        far = first_step(near)
        left = (near[0], shifted(halves[1], 1))
        right = (shifted(halves[0], -1), near[1])
        if early:
            (left, right), early[:] = tied((left, right), early)
        sums = near_sums((halves, left, right), near_spots, gate_own, up_own)
        hidden = far_hidden(far, sums, far_spots, gate_own, up_own)
        return [hidden, shifted(hidden, 1), shifted(hidden, -1), shifted(hidden, 2)]

    def project(chunk, hidden, cost):
        return projected(hidden, down, chunk[1], chunk[2], cost)

    placed = [jnp.where(moved, o, w) for o, w in zip(swaps[:2], own)]
    last = [jnp.where(moved, swapped(own[2]), own[2])]
    halves_a = split(live_rows(CHUNKS[0], got_a))
    hidden_a = activations(halves_a, first_step(halves_a), placed)
    halves_b = split(live_rows(CHUNKS[1], got_b))
    halves_b, hidden_a = tied(halves_b, hidden_a)
    near = first_step(halves_b)
    out_a = project(CHUNKS[0], hidden_a, LONG)
    near, _ = tied(near, out_a)
    back_a = exchanged(out_a)
    hidden_b = activations(halves_b, near, last)
    total, hidden_b = tied(collected(slot_a[:, None], back_a), hidden_b)
    out_b = project(CHUNKS[1], hidden_b, FREE)
    placed += last
    back_b = exchanged(out_b)
    mixed = mixed_rows(slot_b[:, None], back_b, total, gate_weight)
    return (mixed, *placed)


def solution(mesh):
    weights = (P("expert", None, "dp"), P("expert", None, "dp"), P("expert", "dp", None))
    return jax.shard_map(
        body,
        mesh=mesh,
        in_specs=(P("expert", "dp"), P("expert", None), P("expert", None), P(), *weights),
        out_specs=(P("expert", "dp"), *weights),
        check_vma=False,
    )
```
